32 devices in a mesh: pairs: 8 (over y, x, core), fit: 4 (over z).
Axes of the slice: x: 2, y: 2, z: 4, core: 2. Of those that a mesh axis runs over, the one named last changes fastest.
Arguments:
- b_first: bfloat16 [64, 160, 3072], P('pairs', None, 'fit'), may hold values from -0.109375 to 0.109375
- b_second: bfloat16 [64, 160, 3072], P('pairs', None, 'fit'), may hold values from -6 to 6
- start_amplitudes: float32 [64, 160, 160], P('pairs'), may hold values from -1.8 to 1.8
- margins: bfloat16 [64, 96, 160, 160], P('pairs', 'fit'), may hold values from -0.5 to 0.5
- fock_terms: float32 [64, 96], P('pairs', 'fit'), may hold values from -0.2 to 0.2
- partners: int32 [64, 96], P('pairs', 'fit'), may hold values from 0 to 63, as said below
- pno_energy: float32 [64, 160], P('pairs'), may hold values from 0.3 to 1.5
- occ_energy: float32 [4000], replicated, may hold values from -1 to -0.2
- pair_list: int32 [64, 2], P('pairs'), may hold values from 0 to 3999
- pno_count: int32 [64], P('pairs'), may hold values from 64 to 160, as said below
Outputs:
- amplitudes: float32 [64, 160, 160], P('pairs')
- residual: float32 [64, 160, 160], P('pairs')
The draws below stay inside these ranges and needn't reach their ends.
Inputs may be any that keep to these rules, and one draw needn't show every extreme that they name: `pno_count`: each pair's PNO count is one of 64, 128 and 160. `partners`: pairs owner * 8 to owner * 8 + 7 belong to one owner. In the block of one device (its 8 rows and the columns of its index along fit), each owner's pairs appear at most 48 times, and one owner's pairs appear exactly 48 times in every block.
All inputs are finite; a program needn't handle non-finite values.
Results may differ from the reference program's by a relative error of at most 0.0041.
Values may be sent and summed in bfloat16 or wider, within the bound.
A program may use at most 192 MiB of HBM per device.

```python
from functools import partial
import jax
import jax.numpy as jnp
from jax import lax

NPNO = 160
FIT = 3072
NOCC = 4000
PARTNERS = 96
ITERS = 2
PAIR_DEV = 8
PAIRS = 64
N_PAIRS = 8
N_FIT = 4


def block_partners(common_owner, key):
    order_key, pick_key, local_key = jax.random.split(key, 3)
    request_count = PAIR_DEV * PARTNERS // N_FIT
    capacity = 2 * request_count // N_PAIRS
    slot_owner = jnp.arange(N_PAIRS * capacity, dtype=jnp.int32) // capacity
    rotated = (slot_owner + common_owner) % N_PAIRS
    remaining = jax.random.permutation(order_key, rotated[capacity:])
    chosen = jnp.concatenate([rotated[:capacity], remaining])[:request_count]
    chosen = jax.random.permutation(pick_key, chosen)
    local_index = jax.random.randint(local_key, (request_count,), 0, PAIR_DEV)
    return (chosen * PAIR_DEV + local_index).reshape(PAIR_DEV, PARTNERS // N_FIT)


def draw_partners(key, part):
    common_owner = jax.random.randint(jax.random.fold_in(key, 7), (), 0, N_PAIRS)
    block_keys = jax.random.split(jax.random.fold_in(key, 11), N_PAIRS * N_FIT)
    blocks = jax.vmap(lambda single: block_partners(common_owner, single))(block_keys)
    blocks = blocks.reshape(N_PAIRS, N_FIT, PAIR_DEV, PARTNERS // N_FIT)
    return jnp.transpose(blocks, (0, 2, 1, 3)).reshape(PAIRS, PARTNERS).astype(jnp.int32)


def draw_pno_count(key, part):
    level_index = jax.random.randint(jax.random.fold_in(key, 3), (PAIRS,), 0, 3)
    level_table = jnp.array([NPNO * 2 // 5, NPNO * 4 // 5, NPNO], dtype=jnp.int32)
    return level_table[level_index]


def touch_ends(result, own_key, least, largest):
    index_at = [jax.random.randint(jax.random.fold_in(own_key, axis), (), 0, length) for axis, length in enumerate(result.shape)]
    longest = result.shape.index(max(result.shape))
    next_to = index_at[:longest] + [(index_at[longest] + 1) % result.shape[longest]] + index_at[longest + 1:]
    return result.at[tuple(index_at)].set(least).at[tuple(next_to)].set(largest)


def level_of(rng, extent, shards, least, largest):
    factor_of = 1.0
    for position, parts in shards:
        draws = jax.random.uniform(jax.random.fold_in(jax.random.fold_in(rng, 6), position), (parts,), jnp.float32, least / len(shards), largest / len(shards))
        factor_of = factor_of * jnp.repeat(jnp.exp(draws), extent[position] // parts).reshape((-1,) + (1,) * (len(extent) - 1 - position))
    return factor_of


def bell_draw(key, shape, scale, reach, cuts=(), held_as=jnp.bfloat16):
    loudness = level_of(key, shape, cuts, -0.22, 0.18) if cuts else 1.0
    entries = jax.random.normal(key, shape, jnp.float32) * scale * loudness
    return jnp.minimum(jnp.maximum(entries, -reach), reach).astype(held_as)


def setup_inputs(seed: int = 0) -> dict:
    splits = jax.random.split(jax.random.key(seed), 11)
    return {
        "b_first": bell_draw(splits[0], (PAIRS, NPNO, FIT), FIT ** -0.5, 0.109375, ((0, 8), (2, 4))),
        "b_second": bell_draw(splits[1], (PAIRS, NPNO, FIT), 1.0, 6.0, ((0, 8), (2, 4))),
        "start_amplitudes": bell_draw(splits[2], (PAIRS, NPNO, NPNO), 0.3, 1.8, ((0, 8),), jnp.float32),
        "margins": bell_draw(splits[3], (PAIRS, PARTNERS, NPNO, NPNO), NPNO ** -0.5, 0.5, ((0, 8), (1, 4))),
        "fock_terms": jnp.clip(jax.random.uniform(splits[4], (PAIRS, PARTNERS), jnp.float32, -0.2, 0.2) * level_of(splits[4], (PAIRS, PARTNERS), ((0, 8), (1, 4)), -0.4, 0.0), -0.2, 0.2),
        "partners": draw_partners(jax.random.fold_in(splits[10], 71), 0),
        "pno_energy": jnp.clip(0.3 + 1.2 * jax.random.uniform(splits[6], (PAIRS, NPNO), jnp.float32) ** level_of(splits[6], (PAIRS, NPNO), ((0, 8),), -0.2, 0.2), 0.3, 1.5),
        "occ_energy": jnp.clip(jax.random.uniform(splits[7], (NOCC,), jnp.float32, -1.0, -0.2), -1.0, -0.2),
        "pair_list": touch_ends(jax.random.randint(splits[8], (PAIRS, 2), 0, NOCC), jax.random.fold_in(splits[8], 1), 0, NOCC - 1).astype(jnp.int32),
        "pno_count": draw_pno_count(jax.random.fold_in(splits[10], 71), 0),
    }


def pair_coupling(rounded, pieces):
    margin_rows, fock_row, partner_row = pieces
    fetched = rounded[partner_row].astype(jnp.float32)
    margin_block = margin_rows.astype(jnp.float32)
    left_product = jnp.einsum("pac,pcd->pad", margin_block, fetched, precision=lax.Precision.HIGHEST)
    left_product = lax.optimization_barrier(left_product.astype(jnp.bfloat16)).astype(jnp.float32)
    right_product = jnp.einsum("pad,pbd->pab", left_product, margin_block, precision=lax.Precision.HIGHEST)
    return jnp.sum(fock_row[:, None, None] * right_product, axis=0)


def pair_integrals(pieces):
    return jnp.dot(pieces[0], pieces[1].T, preferred_element_type=jnp.float32)


def reference(b_first, b_second, start_amplitudes, margins, fock_terms, partners, pno_energy, occ_energy, pair_list, pno_count):
    levels = jnp.arange(NPNO, dtype=jnp.int32)
    keep_rows = (levels[None, :] < pno_count[:, None]).astype(jnp.float32)
    pair_mask = keep_rows[:, :, None] * keep_rows[:, None, :]
    occ_pair = occ_energy[pair_list[:, 0]] + occ_energy[pair_list[:, 1]]
    denominator = pno_energy[:, :, None] + pno_energy[:, None, :] - occ_pair[:, None, None]
    integrals = lax.map(pair_integrals, (b_first, b_second))
    amplitudes = pair_mask * start_amplitudes
    residual = jnp.zeros_like(amplitudes)
    for iteration in range(ITERS):
        rounded = amplitudes.astype(jnp.bfloat16)
        coupling = lax.map(partial(pair_coupling, rounded), (margins, fock_terms, partners))
        residual = pair_mask * (integrals - coupling + denominator * amplitudes)
        amplitudes = amplitudes - residual / denominator
    return amplitudes, residual
```

```python
import functools
import jax
import jax.numpy as jnp
from jax import lax
from jax.experimental import pallas as pl
from jax.experimental.pallas import tpu as pltpu
from jax.sharding import PartitionSpec as P

ITERS = 2
LANES = 128
BF16 = jnp.bfloat16
F32 = jnp.float32


def kernel(
    n_pairs,
    n_fit,
    start_ref,
    energy_ref,
    fock_ref,
    partner_ref,
    occ_ref,
    list_ref,
    count_ref,
    b_first_ref,
    b_second_ref,
    margins_ref,
    amp_out,
    res_out,
    margins,
    first,
    second,
    gathered,
    everything,
    amp_own,
    int_send,
    int_recv,
    coup_send,
    coup_recv,
    low,
    res_all,
    margin_sem,
    b_sem,
    gat_send,
    gat_fwd,
    gat_recv,
    fit_send,
    fit_recv,
    free_sem,
):
    int_own, coup_own = amp_out, res_out
    me = lax.axis_index("pairs")
    z = lax.axis_index("fit")
    chips = n_pairs // 2
    chip, core = me // 2, lax.rem(me, 2)
    sibling = chip * 2 + (1 - core)
    pair_dev, width, _ = start_ref.shape
    per_pair = margins.shape[1]
    own_pairs = pair_dev // n_fit
    tail = width - LANES
    fold = LANES // (tail * own_pairs)
    tail_rows = width // fold
    tail_at = own_pairs * width

    def margin_copy(row):
        return pltpu.make_async_copy(
            margins_ref.at[row], margins.at[row], margin_sem.at[row]
        )

    copy_first = pltpu.make_async_copy(b_first_ref, first, b_sem.at[0])
    copy_second = pltpu.make_async_copy(b_second_ref, second, b_sem.at[1])
    copy_first.start()
    copy_second.start()
    for row in range(pair_dev):
        margin_copy(row).start()

    barrier = pltpu.get_barrier_semaphore()

    def same_core(step):
        return lax.rem(chip + step, chips) * 2 + core

    def greet(sem):
        @pl.loop(1, chips)
        def _(step):
            pl.semaphore_signal(
                sem, inc=1, device_id={"pairs": same_core(step), "fit": z}
            )

        pl.semaphore_signal(sem, inc=1, device_id={"pairs": sibling, "fit": z})
        for step in range(1, n_fit):
            pl.semaphore_signal(
                sem,
                inc=1,
                device_id={"pairs": me, "fit": lax.rem(z + step, n_fit)},
            )

    greeted = chips - 1 + 1 + n_fit - 1
    greet(barrier)

    def pack(ref, blocks):
        for index, block in enumerate(blocks):
            ref[pl.ds(index * width, width), :] = block[:, :LANES].astype(ref.dtype)
        pieces = []
        for part in range(fold):
            for block in blocks:
                pieces.append(
                    block[part * tail_rows : (part + 1) * tail_rows, LANES:]
                )
        ref[pl.ds(tail_at, tail_rows), :] = jnp.concatenate(pieces, axis=1).astype(
            ref.dtype
        )

    def unpack_tail(ref, index):
        lanes = ref[pl.ds(tail_at, tail_rows), :].astype(F32)
        pieces = []
        for part in range(fold):
            at = (part * own_pairs + index) * tail
            pieces.append(lanes[:, at : at + tail])
        return jnp.concatenate(pieces, axis=0)

    def unpack(ref, index):
        main = ref[pl.ds(index * width, width), :].astype(F32)
        return jnp.concatenate([main, unpack_tail(ref, index)], axis=1)

    rows_at = lax.broadcasted_iota(jnp.int32, (width, width), 0)
    cols_at = lax.broadcasted_iota(jnp.int32, (width, width), 1)

    def mask_of(row):
        count = count_ref[row]
        keep = (rows_at < count).astype(F32) * (cols_at < count).astype(F32)
        return keep

    orbitals = lax.broadcasted_iota(jnp.int32, occ_ref.shape, 1)

    def occ_of(orbital):
        return jnp.sum(
            jnp.where(orbitals == orbital, occ_ref[...], 0.0), axis=1, keepdims=True
        )

    def denominator_of(row):
        across = jnp.broadcast_to(energy_ref[pl.ds(row, 1), :], (width, width))
        down = jnp.sum(
            jnp.where(rows_at == cols_at, across, 0.0), axis=1, keepdims=True
        )
        return down + across - (occ_of(list_ref[row, 0]) + occ_of(list_ref[row, 1]))

    @pl.loop(0, n_fit)
    def _(part):
        pack(
            gathered.at[me * n_fit + part],
            [
                mask_of(part * own_pairs + index) * start_ref[part * own_pairs + index]
                for index in range(own_pairs)
            ],
        )

    for index in range(own_pairs):
        row = z * own_pairs + index
        amp_own[index] = mask_of(row) * start_ref[row]

    pl.semaphore_wait(barrier, greeted)

    def direct(owner, part, step, target):
        slot = owner * n_fit + part
        return pltpu.make_async_remote_copy(
            src_ref=gathered.at[slot],
            dst_ref=gathered.at[slot],
            send_sem=gat_send.at[step, part],
            recv_sem=gat_recv.at[slot],
            device_id={"pairs": target, "fit": z},
        )

    def forward(owner, part):
        slot = owner * n_fit + part
        return pltpu.make_async_remote_copy(
            src_ref=gathered.at[slot],
            dst_ref=gathered.at[slot],
            send_sem=gat_fwd.at[slot],
            recv_sem=gat_recv.at[slot],
            device_id={"pairs": sibling, "fit": z},
        )

    def send_part(part):
        @pl.loop(1, chips)
        def _(step):
            direct(me, part, step, same_core(step)).start()

        forward(me, part).start()

    def fill(owner, part):
        slot = owner * n_fit + part
        for index in range(own_pairs):
            everything[slot * own_pairs + index] = unpack(
                gathered.at[slot], index
            ).astype(BF16)

    def part_at(step):
        return lax.rem(z + step, n_fit)

    def collect():
        @pl.loop(0, n_fit)
        def _(turn):
            part = part_at(turn)
            fill(me, part)

            @pl.loop(1, chips)
            def _(step):
                owner = same_core(chips - step)
                direct(owner, part, step, me).wait_recv()
                forward(owner, part).start()
                fill(owner, part)

        @pl.loop(0, n_fit)
        def _(turn):
            part = part_at(turn)

            @pl.loop(0, chips)
            def _(step):
                owner = lax.rem(chip + chips - step, chips) * 2 + (1 - core)
                forward(owner, part).wait_recv()
                fill(owner, part)

    def finish_sends():
        @pl.loop(0, n_fit)
        def _(part):
            @pl.loop(1, chips)
            def _(step):
                direct(me, part, step, same_core(step)).wait_send()
                forward(same_core(step), part).wait_send()

            forward(me, part).wait_send()

    def fit_copy(kind, step, source, target_ref):
        return pltpu.make_async_remote_copy(
            src_ref=source,
            dst_ref=target_ref,
            send_sem=fit_send.at[kind, step],
            recv_sem=fit_recv.at[kind, step],
            device_id={"pairs": me, "fit": part_at(step)},
        )

    def scatter_copy(kind, step, send, recv):
        return fit_copy(kind, step, send.at[step], recv.at[step])

    def spread_copy(kind, step, buffer, slot):
        return fit_copy(kind, step, buffer.at[slot], buffer.at[slot])

    def couple(row):
        coup_own[row] = jnp.zeros((width, width), F32)

        @pl.loop(0, per_pair // GROUP)
        def _(turn):
            total = None
            for inner in range(GROUP):
                col = turn * GROUP + inner
                partner = partner_ref[row, col]
                margin = margins[row, col]
                left = jnp.dot(
                    margin, everything[partner], preferred_element_type=F32
                ).astype(BF16)
                right = lax.dot_general(
                    left,
                    margin,
                    (((1,), (1,)), ((), ())),
                    preferred_element_type=F32,
                )
                term = fock_ref[row, col] * right
                total = term if total is None else total + term
            coup_own[row] = coup_own[row] + total

    INT, COUP, HIGH, LOW, RES = 0, 1, 3, 4, 5

    @pl.loop(0, n_fit)
    def _(part):
        send_part(part_at(part))

    copy_first.wait()
    copy_second.wait()

    def integrals_of(row):
        return lax.dot_general(
            first[row],
            second[row],
            (((1,), (1,)), ((), ())),
            preferred_element_type=F32,
        )

    @pl.loop(1, n_fit)
    def _(step):
        part = part_at(step)
        pack(
            int_send.at[step],
            [integrals_of(part * own_pairs + index) for index in range(own_pairs)],
        )
        scatter_copy(INT, step, int_send, int_recv).start()

    for index in range(own_pairs):
        int_own[index] = integrals_of(z * own_pairs + index)

    collect()

    for iteration in range(ITERS):
        if iteration == 0:
            for row in range(pair_dev):
                margin_copy(row).wait()
        sent = coup_send.at[iteration]
        got = coup_recv.at[iteration]

        @pl.loop(1, n_fit)
        def _(step):
            part = part_at(step)
            for index in range(own_pairs):
                couple(part * own_pairs + index)
            pack(
                sent.at[step],
                [coup_own[part * own_pairs + index] for index in range(own_pairs)],
            )
            scatter_copy(COUP + iteration, step, sent, got).start()

        for index in range(own_pairs):
            couple(z * own_pairs + index)

        if iteration == 0:
            finish_sends()
            greet(free_sem)

            @pl.loop(1, n_fit)
            def _(step):
                scatter_copy(INT, step, int_send, int_recv).wait()
                for index in range(own_pairs):
                    int_own[index] = int_own[index] + unpack(int_recv.at[step], index)

        @pl.loop(1, n_fit)
        def _(step):
            scatter_copy(COUP + iteration, step, sent, got).wait()
            for index in range(own_pairs):
                row = z * own_pairs + index
                coup_own[row] = coup_own[row] + unpack(got.at[step], index)

        updated, residuals = [], []
        for index in range(own_pairs):
            row = z * own_pairs + index
            denominator = denominator_of(row)
            amplitudes = amp_own[index]
            residual = mask_of(row) * (
                int_own[index] - coup_own[row] + denominator * amplitudes
            )
            residuals.append(residual)
            updated.append(amplitudes - residual / denominator)

        if iteration < ITERS - 1:
            pl.semaphore_wait(free_sem, greeted)
            mine = me * n_fit + z
            pack(gathered.at[mine], updated)
            pack(
                low.at[z],
                [block - block.astype(BF16).astype(F32) for block in updated],
            )
            for step in range(1, n_fit):
                spread_copy(HIGH, step, gathered, mine).start()
            send_part(z)
            for step in range(1, n_fit):
                spread_copy(LOW, step, low, z).start()
            for index in range(own_pairs):
                amp_own[index] = updated[index]

            @pl.loop(1, n_fit)
            def _(step):
                part = lax.rem(z + n_fit - step, n_fit)
                spread_copy(HIGH, step, gathered, me * n_fit + part).wait_recv()
                send_part(part)

            collect()
            for step in range(1, n_fit):
                spread_copy(HIGH, step, gathered, mine).wait_send()
        else:
            pack(res_all.at[z], residuals)
            for step in range(1, n_fit):
                spread_copy(RES, step, res_all, z).start()

    finish_sends()
    for step in range(1, n_fit):
        spread_copy(LOW, step, low, z).wait_send()
        part = lax.rem(z + n_fit - step, n_fit)
        spread_copy(LOW, step, low, part).wait_recv()

    @pl.loop(0, n_fit)
    def _(step):
        part = lax.rem(z + n_fit - step, n_fit)

        @pl.when(step > 0)
        def _():
            spread_copy(RES, step, res_all, part).wait_recv()

        for index in range(own_pairs):
            row = part * own_pairs + index
            residual = unpack(res_all.at[part], index)
            amplitudes = unpack(gathered.at[me * n_fit + part], index) + unpack(
                low.at[part], index
            )
            res_out[row] = residual
            amp_out[row] = amplitudes - residual / denominator_of(row)

    for step in range(1, n_fit):
        spread_copy(RES, step, res_all, z).wait_send()


GROUP = 4


def shards(
    n_pairs,
    n_fit,
    b_first,
    b_second,
    start_amplitudes,
    margins,
    fock_terms,
    partners,
    pno_energy,
    occ_energy,
    pair_list,
    pno_count,
):
    pair_dev, width, _ = start_amplitudes.shape
    own_pairs = pair_dev // n_fit
    tail = width - LANES
    packed = (own_pairs * width + own_pairs * width * tail // LANES, LANES)
    slots = n_pairs * n_fit
    out = jax.ShapeDtypeStruct(start_amplitudes.shape, F32)
    vmem = pl.BlockSpec(memory_space=pltpu.VMEM)
    smem = pl.BlockSpec(memory_space=pltpu.SMEM)
    hbm = pl.BlockSpec(memory_space=pl.ANY)
    return pl.pallas_call(
        functools.partial(kernel, n_pairs, n_fit),
        out_shape=(out, out),
        in_specs=[vmem, vmem, smem, smem, vmem, smem, smem, hbm, hbm, hbm],
        out_specs=(vmem, vmem),
        scratch_shapes=[
            pltpu.VMEM(margins.shape, BF16),
            pltpu.VMEM(b_first.shape, BF16),
            pltpu.VMEM(b_second.shape, BF16),
            pltpu.VMEM((slots,) + packed, BF16),
            pltpu.VMEM((n_pairs * pair_dev, width, width), BF16),
            pltpu.VMEM((own_pairs, width, width), F32),
            pltpu.VMEM((n_fit,) + packed, F32),
            pltpu.VMEM((n_fit,) + packed, F32),
            pltpu.VMEM((ITERS, n_fit) + packed, BF16),
            pltpu.VMEM((ITERS, n_fit) + packed, BF16),
            pltpu.VMEM((n_fit,) + packed, BF16),
            pltpu.VMEM((n_fit,) + packed, BF16),
            pltpu.SemaphoreType.DMA((pair_dev,)),
            pltpu.SemaphoreType.DMA((2,)),
            pltpu.SemaphoreType.DMA((n_pairs // 2, n_fit)),
            pltpu.SemaphoreType.DMA((slots,)),
            pltpu.SemaphoreType.DMA((slots,)),
            pltpu.SemaphoreType.DMA((6, n_fit)),
            pltpu.SemaphoreType.DMA((6, n_fit)),
            pltpu.SemaphoreType.REGULAR,
        ],
        compiler_params=pltpu.CompilerParams(
            collective_id=0, has_side_effects=True, vmem_limit_bytes=65000 * 1024
        ),
    )(
        start_amplitudes,
        pno_energy,
        fock_terms,
        partners,
        occ_energy.reshape(1, -1),
        pair_list,
        pno_count,
        b_first,
        b_second,
        margins,
    )


def solution(mesh):
    return jax.shard_map(
        functools.partial(shards, mesh.shape["pairs"], mesh.shape["fit"]),
        mesh=mesh,
        in_specs=(
            P("pairs", None, "fit"),
            P("pairs", None, "fit"),
            P("pairs", None, None),
            P("pairs", "fit", None, None),
            P("pairs", "fit"),
            P("pairs", "fit"),
            P("pairs", None),
            P(),
            P("pairs", None),
            P("pairs"),
        ),
        out_specs=(P("pairs", None, None), P("pairs", None, None)),
        check_vma=False,
    )
```

```python
import functools
import jax
import jax.numpy as jnp
from jax import lax
from jax.experimental import pallas as pl
from jax.experimental.pallas import tpu as pltpu
from jax.sharding import PartitionSpec as P

ITERS = 2
LANES = 128
BF16 = jnp.bfloat16
F32 = jnp.float32


def flip(value, bits, size):
    result, place = 0, 1
    while place < size:
        one = (value // place) % 2
        other = (bits // place) % 2
        result = result + place * ((one + other) % 2)
        place *= 2
    return result


def kernel(
    n_pairs,
    n_fit,
    start_ref,
    energy_ref,
    fock_ref,
    partner_ref,
    occ_ref,
    list_ref,
    count_ref,
    b_first_ref,
    b_second_ref,
    margins_ref,
    amp_out,
    res_out,
    margins,
    first,
    second,
    gathered,
    everything,
    amp_own,
    denom,
    int_send,
    int_recv,
    coup_send,
    coup_recv,
    low,
    res_all,
    margin_sem,
    b_sem,
    gat_send,
    gat_fwd,
    gat_relay,
    gat_recv,
    fit_send,
    fit_recv,
    free_sem,
):
    int_own, coup_own = amp_out, res_out
    me = lax.axis_index("pairs")
    z = lax.axis_index("fit")
    chips = n_pairs // 2
    chip, core = me // 2, lax.rem(me, 2)
    sibling = chip * 2 + (1 - core)
    pair_dev, width, _ = start_ref.shape
    per_pair = margins.shape[1]
    own_pairs = pair_dev // n_fit
    tail = width - LANES
    fold = LANES // (tail * own_pairs)
    tail_rows = width // fold
    tail_at = own_pairs * width

    def margin_copy(row):
        return pltpu.make_async_copy(
            margins_ref.at[row], margins.at[row], margin_sem.at[row]
        )

    copy_first = pltpu.make_async_copy(b_first_ref, first, b_sem.at[0])
    copy_second = pltpu.make_async_copy(b_second_ref, second, b_sem.at[1])
    copy_first.start()
    copy_second.start()
    for row in range(pair_dev):
        margin_copy(row).start()

    barrier = pltpu.get_barrier_semaphore()

    def same_core(step):
        return lax.rem(chip + step, chips) * 2 + core

    def part_at(step):
        if n_fit & (n_fit - 1):
            return lax.rem(2 * n_fit - z - step, n_fit)
        return flip(z, step, n_fit)

    def greet(sem):
        @pl.loop(1, chips)
        def _(step):
            pl.semaphore_signal(
                sem, inc=1, device_id={"pairs": same_core(step), "fit": z}
            )

        pl.semaphore_signal(sem, inc=1, device_id={"pairs": sibling, "fit": z})
        for step in range(1, n_fit):
            pl.semaphore_signal(
                sem,
                inc=1,
                device_id={"pairs": me, "fit": part_at(step)},
            )

    greeted = chips - 1 + 1 + n_fit - 1
    greet(barrier)

    def pack(ref, blocks):
        for index, block in enumerate(blocks):
            ref[pl.ds(index * width, width), :] = block[:, :LANES].astype(ref.dtype)
        pieces = []
        for part in range(fold):
            for block in blocks:
                pieces.append(
                    block[part * tail_rows : (part + 1) * tail_rows, LANES:]
                )
        ref[pl.ds(tail_at, tail_rows), :] = jnp.concatenate(pieces, axis=1).astype(
            ref.dtype
        )

    def unpack_tail(ref, index):
        lanes = ref[pl.ds(tail_at, tail_rows), :].astype(F32)
        pieces = []
        for part in range(fold):
            at = (part * own_pairs + index) * tail
            pieces.append(lanes[:, at : at + tail])
        return jnp.concatenate(pieces, axis=0)

    def unpack(ref, index):
        main = ref[pl.ds(index * width, width), :].astype(F32)
        return jnp.concatenate([main, unpack_tail(ref, index)], axis=1)

    rows_at = lax.broadcasted_iota(jnp.int32, (width, width), 0)
    cols_at = lax.broadcasted_iota(jnp.int32, (width, width), 1)

    def mask_of(row):
        count = count_ref[row]
        keep = (rows_at < count).astype(F32) * (cols_at < count).astype(F32)
        return keep

    orbitals = lax.broadcasted_iota(jnp.int32, occ_ref.shape, 1)

    def occ_of(orbital):
        return jnp.sum(
            jnp.where(orbitals == orbital, occ_ref[...], 0.0), axis=1, keepdims=True
        )

    def denominator_of(row):
        across = jnp.broadcast_to(energy_ref[pl.ds(row, 1), :], (width, width))
        down = jnp.sum(
            jnp.where(rows_at == cols_at, across, 0.0), axis=1, keepdims=True
        )
        return down + across - (occ_of(list_ref[0, row]) + occ_of(list_ref[1, row]))

    @pl.loop(0, n_fit)
    def _(part):
        pack(
            gathered.at[me * n_fit + part],
            [
                mask_of(part * own_pairs + index) * start_ref[part * own_pairs + index]
                for index in range(own_pairs)
            ],
        )

    for index in range(own_pairs):
        row = z * own_pairs + index
        amp_own[index] = mask_of(row) * start_ref[row]

    pl.semaphore_wait(barrier, greeted)

    def direct(owner, part, step, target):
        slot = owner * n_fit + part
        return pltpu.make_async_remote_copy(
            src_ref=gathered.at[slot],
            dst_ref=gathered.at[slot],
            send_sem=gat_send.at[step, part],
            recv_sem=gat_recv.at[slot],
            device_id={"pairs": target, "fit": z},
        )

    def forward(owner, part):
        slot = owner * n_fit + part
        return pltpu.make_async_remote_copy(
            src_ref=gathered.at[slot],
            dst_ref=gathered.at[slot],
            send_sem=gat_fwd.at[slot],
            recv_sem=gat_recv.at[slot],
            device_id={"pairs": sibling, "fit": z},
        )

    relayed = chips == 4
    near = (1, 2) if relayed else ()

    def at_chip(step):
        return flip(chip, step, chips) * 2 + core

    def relay(owner, part, step):
        slot = owner * n_fit + part
        return pltpu.make_async_remote_copy(
            src_ref=gathered.at[slot],
            dst_ref=gathered.at[slot],
            send_sem=gat_relay.at[slot],
            recv_sem=gat_recv.at[slot],
            device_id={"pairs": at_chip(step), "fit": z},
        )

    def send_part(part):
        if relayed:
            for step in near:
                direct(me, part, step, at_chip(step)).start()
        else:

            @pl.loop(1, chips)
            def _(step):
                direct(me, part, step, same_core(step)).start()

        forward(me, part).start()

    def fill(owner, part):
        slot = owner * n_fit + part
        for index in range(own_pairs):
            everything[slot * own_pairs + index] = unpack(
                gathered.at[slot], index
            ).astype(BF16)

    def take_direct(turn):
        part = part_at(turn)
        if relayed:
            for step in near:
                owner = at_chip(step)
                direct(owner, part, step, me).wait_recv()
                if step - 1 == turn % 2:
                    relay(owner, part, 3 - step).start()
                forward(owner, part).start()
            fill(me, part)
            for step in near:
                fill(at_chip(step), part)
        else:
            fill(me, part)

            @pl.loop(1, chips)
            def _(step):
                owner = same_core(chips - step)
                direct(owner, part, step, me).wait_recv()
                forward(owner, part).start()
                fill(owner, part)

    def take_far(turn):
        part = part_at(turn)
        if relayed:
            owner = at_chip(3)
            direct(owner, part, 1, me).wait_recv()
            forward(owner, part).start()
            fill(owner, part)

    def take_sibling():
        @pl.loop(0, n_fit)
        def _(turn):
            part = part_at(turn)

            @pl.loop(0, chips)
            def _(step):
                owner = lax.rem(chip + chips - step, chips) * 2 + (1 - core)
                forward(owner, part).wait_recv()
                fill(owner, part)

    def finish_sends():
        if relayed:
            for turn in range(n_fit):
                part = part_at(turn)
                for step in near:
                    direct(me, part, step, at_chip(step)).wait_send()
                    if step - 1 == turn % 2:
                        relay(at_chip(step), part, 3 - step).wait_send()

        @pl.loop(0, n_fit)
        def _(part):
            @pl.loop(1, chips)
            def _(step):
                if not relayed:
                    direct(me, part, step, same_core(step)).wait_send()
                forward(same_core(step), part).wait_send()

            forward(me, part).wait_send()

    def fit_copy(kind, step, source, target_ref):
        return pltpu.make_async_remote_copy(
            src_ref=source,
            dst_ref=target_ref,
            send_sem=fit_send.at[kind, step],
            recv_sem=fit_recv.at[kind, step],
            device_id={"pairs": me, "fit": part_at(step)},
        )

    def scatter_copy(kind, step, send, recv):
        return fit_copy(kind, step, send.at[step], recv.at[step])

    def spread_copy(kind, step, buffer, slot):
        return fit_copy(kind, step, buffer.at[slot], buffer.at[slot])

    def couple(row):
        coup_own[row] = jnp.zeros((width, width), F32)

        @pl.loop(0, per_pair // GROUP)
        def _(turn):
            total = None
            for inner in range(GROUP):
                col = turn * GROUP + inner
                partner = partner_ref[row, col]
                margin = margins[row, col]
                left = jnp.dot(
                    margin, everything[partner], preferred_element_type=F32
                ).astype(BF16)
                right = lax.dot_general(
                    left,
                    margin,
                    (((1,), (1,)), ((), ())),
                    preferred_element_type=F32,
                )
                term = fock_ref[row, col] * right
                total = term if total is None else total + term
            coup_own[row] = coup_own[row] + total

    INT, COUP, HIGH, LOW, RES = 0, 1, 3, 4, 5

    @pl.loop(0, n_fit)
    def _(part):
        send_part(part_at(part))

    copy_first.wait()
    copy_second.wait()

    def integrals_of(row):
        return lax.dot_general(
            first[row],
            second[row],
            (((1,), (1,)), ((), ())),
            preferred_element_type=F32,
        )

    @pl.loop(1, n_fit)
    def _(step):
        part = part_at(step)
        pack(
            int_send.at[step],
            [integrals_of(part * own_pairs + index) for index in range(own_pairs)],
        )
        scatter_copy(INT, step, int_send, int_recv).start()

    for index in range(own_pairs):
        int_own[index] = integrals_of(z * own_pairs + index)

    @pl.loop(0, pair_dev)
    def _(row):
        denom[row] = denominator_of(row)

    for turn in range(n_fit):
        take_direct(turn)
    for turn in range(n_fit):
        take_far(turn)
    take_sibling()

    for iteration in range(ITERS):
        if iteration == 0:
            for row in range(pair_dev):
                margin_copy(row).wait()
        sent = coup_send.at[iteration]
        got = coup_recv.at[iteration]

        @pl.loop(1, n_fit)
        def _(turn):
            step = n_fit - turn
            part = part_at(step)
            for index in range(own_pairs):
                couple(part * own_pairs + index)
            pack(
                sent.at[step],
                [coup_own[part * own_pairs + index] for index in range(own_pairs)],
            )
            scatter_copy(COUP + iteration, step, sent, got).start()

        for index in range(own_pairs):
            couple(z * own_pairs + index)

        if iteration == 0:
            finish_sends()
            greet(free_sem)

            @pl.loop(1, n_fit)
            def _(step):
                scatter_copy(INT, step, int_send, int_recv).wait()
                for index in range(own_pairs):
                    int_own[index] = int_own[index] + unpack(int_recv.at[step], index)

        @pl.loop(1, n_fit)
        def _(step):
            scatter_copy(COUP + iteration, step, sent, got).wait()
            for index in range(own_pairs):
                row = z * own_pairs + index
                coup_own[row] = coup_own[row] + unpack(got.at[step], index)

        updated, residuals = [], []
        for index in range(own_pairs):
            row = z * own_pairs + index
            denominator = denom[row]
            amplitudes = amp_own[index]
            residual = mask_of(row) * (
                int_own[index] - coup_own[row] + denominator * amplitudes
            )
            residuals.append(residual)
            updated.append(amplitudes - residual / denominator)

        if iteration < ITERS - 1:
            pl.semaphore_wait(free_sem, greeted)
            mine = me * n_fit + z
            pack(gathered.at[mine], updated)
            pack(
                low.at[z],
                [block - block.astype(BF16).astype(F32) for block in updated],
            )
            for step in range(1, n_fit):
                spread_copy(HIGH, step, gathered, mine).start()
            send_part(z)
            for step in range(1, n_fit):
                spread_copy(LOW, step, low, z).start()
            for index in range(own_pairs):
                amp_own[index] = updated[index]

            for turn in range(1, n_fit):
                part = part_at(turn)
                spread_copy(HIGH, turn, gathered, me * n_fit + part).wait_recv()
                send_part(part)
                take_direct(turn - 1)
                if turn > 1:
                    take_far(turn - 2)
            take_direct(n_fit - 1)
            for turn in range(max(n_fit - 2, 0), n_fit):
                take_far(turn)
            take_sibling()
            for step in range(1, n_fit):
                spread_copy(HIGH, step, gathered, mine).wait_send()
        else:
            pack(res_all.at[z], residuals)
            for step in range(1, n_fit):
                spread_copy(RES, step, res_all, z).start()

    finish_sends()
    for step in range(1, n_fit):
        spread_copy(LOW, step, low, z).wait_send()
        part = part_at(step)
        spread_copy(LOW, step, low, part).wait_recv()

    @pl.loop(0, n_fit)
    def _(step):
        part = part_at(step)

        @pl.when(step > 0)
        def _():
            spread_copy(RES, step, res_all, part).wait_recv()

        for index in range(own_pairs):
            row = part * own_pairs + index
            residual = unpack(res_all.at[part], index)
            amplitudes = unpack(gathered.at[me * n_fit + part], index) + unpack(
                low.at[part], index
            )
            res_out[row] = residual
            amp_out[row] = amplitudes - residual / denom[row]

    for step in range(1, n_fit):
        spread_copy(RES, step, res_all, z).wait_send()


GROUP = 12


def shards(
    n_pairs,
    n_fit,
    b_first,
    b_second,
    start_amplitudes,
    margins,
    fock_terms,
    partners,
    pno_energy,
    occ_energy,
    pair_list,
    pno_count,
):
    pair_dev, width, _ = start_amplitudes.shape
    own_pairs = pair_dev // n_fit
    tail = width - LANES
    packed = (own_pairs * width + own_pairs * width * tail // LANES, LANES)
    slots = n_pairs * n_fit
    out = jax.ShapeDtypeStruct(start_amplitudes.shape, F32)
    vmem = pl.BlockSpec(memory_space=pltpu.VMEM)
    smem = pl.BlockSpec(memory_space=pltpu.SMEM)
    hbm = pl.BlockSpec(memory_space=pl.ANY)
    return pl.pallas_call(
        functools.partial(kernel, n_pairs, n_fit),
        out_shape=(out, out),
        in_specs=[vmem, vmem, smem, smem, vmem, smem, smem, hbm, hbm, hbm],
        out_specs=(vmem, vmem),
        scratch_shapes=[
            pltpu.VMEM(margins.shape, BF16),
            pltpu.VMEM(b_first.shape, BF16),
            pltpu.VMEM(b_second.shape, BF16),
            pltpu.VMEM((slots,) + packed, BF16),
            pltpu.VMEM((n_pairs * pair_dev, width, width), BF16),
            pltpu.VMEM((own_pairs, width, width), F32),
            pltpu.VMEM((pair_dev, width, width), F32),
            pltpu.VMEM((n_fit,) + packed, F32),
            pltpu.VMEM((n_fit,) + packed, F32),
            pltpu.VMEM((ITERS, n_fit) + packed, BF16),
            pltpu.VMEM((ITERS, n_fit) + packed, BF16),
            pltpu.VMEM((n_fit,) + packed, BF16),
            pltpu.VMEM((n_fit,) + packed, BF16),
            pltpu.SemaphoreType.DMA((pair_dev,)),
            pltpu.SemaphoreType.DMA((2,)),
            pltpu.SemaphoreType.DMA((n_pairs // 2, n_fit)),
            pltpu.SemaphoreType.DMA((slots,)),
            pltpu.SemaphoreType.DMA((slots,)),
            pltpu.SemaphoreType.DMA((slots,)),
            pltpu.SemaphoreType.DMA((6, n_fit)),
            pltpu.SemaphoreType.DMA((6, n_fit)),
            pltpu.SemaphoreType.REGULAR,
        ],
        compiler_params=pltpu.CompilerParams(
            collective_id=0, has_side_effects=True, vmem_limit_bytes=65000 * 1024
        ),
    )(
        start_amplitudes,
        pno_energy,
        fock_terms,
        partners,
        occ_energy.reshape(1, -1),
        pair_list.T,
        pno_count,
        b_first,
        b_second,
        margins,
    )


def solution(mesh):
    return jax.shard_map(
        functools.partial(shards, mesh.shape["pairs"], mesh.shape["fit"]),
        mesh=mesh,
        in_specs=(
            P("pairs", None, "fit"),
            P("pairs", None, "fit"),
            P("pairs", None, None),
            P("pairs", "fit", None, None),
            P("pairs", "fit"),
            P("pairs", "fit"),
            P("pairs", None),
            P(),
            P("pairs", None),
            P("pairs"),
        ),
        out_specs=(P("pairs", None, None), P("pairs", None, None)),
        check_vma=False,
    )
```

```python
import functools
import jax
import jax.numpy as jnp
from jax import lax
from jax.experimental import pallas as pl
from jax.experimental.pallas import tpu as pltpu
from jax.sharding import PartitionSpec as P

ITERS = 2
LANES = 128
BF16 = jnp.bfloat16
F32 = jnp.float32


def flip(value, bits, size):
    result, place = 0, 1
    while place < size:
        one = (value // place) % 2
        other = (bits // place) % 2
        result = result + place * ((one + other) % 2)
        place *= 2
    return result


def kernel(
    n_pairs,
    n_fit,
    start_ref,
    energy_ref,
    fock_ref,
    partner_ref,
    occ_ref,
    list_ref,
    count_ref,
    b_first_ref,
    b_second_ref,
    margins_ref,
    amp_out,
    res_out,
    margins,
    first,
    second,
    gathered,
    everything,
    amp_own,
    denom,
    int_send,
    int_recv,
    coup_send,
    coup_recv,
    low,
    res_all,
    margin_sem,
    b_sem,
    gat_send,
    gat_fwd,
    gat_relay,
    gat_recv,
    fit_send,
    fit_recv,
    free_sem,
):
    int_own, coup_own = amp_out, res_out
    me = lax.axis_index("pairs")
    z = lax.axis_index("fit")
    chips = n_pairs // 2
    chip, core = me // 2, lax.rem(me, 2)
    sibling = chip * 2 + (1 - core)
    pair_dev, width, _ = start_ref.shape
    per_pair = margins.shape[1]
    own_pairs = pair_dev // n_fit
    tail = width - LANES
    fold = LANES // (tail * own_pairs)
    tail_rows = width // fold
    tail_at = own_pairs * width

    def margin_copy(row):
        return pltpu.make_async_copy(
            margins_ref.at[row], margins.at[row], margin_sem.at[row]
        )

    copy_first = pltpu.make_async_copy(b_first_ref, first, b_sem.at[0])
    copy_second = pltpu.make_async_copy(b_second_ref, second, b_sem.at[1])
    copy_first.start()
    copy_second.start()
    for row in range(pair_dev):
        margin_copy(row).start()

    barrier = pltpu.get_barrier_semaphore()

    def same_core(step):
        return lax.rem(chip + step, chips) * 2 + core

    def part_at(step):
        if n_fit & (n_fit - 1):
            return lax.rem(2 * n_fit - z - step, n_fit)
        return flip(z, step, n_fit)

    def greet(sem):
        @pl.loop(1, chips)
        def _(step):
            pl.semaphore_signal(
                sem, inc=1, device_id={"pairs": same_core(step), "fit": z}
            )

        pl.semaphore_signal(sem, inc=1, device_id={"pairs": sibling, "fit": z})
        for step in range(1, n_fit):
            pl.semaphore_signal(
                sem,
                inc=1,
                device_id={"pairs": me, "fit": part_at(step)},
            )

    greeted = chips - 1 + 1 + n_fit - 1
    greet(barrier)

    def pack(ref, blocks):
        for index, block in enumerate(blocks):
            ref[pl.ds(index * width, width), :] = block[:, :LANES].astype(ref.dtype)
        pieces = []
        for part in range(fold):
            for block in blocks:
                pieces.append(
                    block[part * tail_rows : (part + 1) * tail_rows, LANES:]
                )
        ref[pl.ds(tail_at, tail_rows), :] = jnp.concatenate(pieces, axis=1).astype(
            ref.dtype
        )

    def unpack_tail(ref, index):
        lanes = ref[pl.ds(tail_at, tail_rows), :].astype(F32)
        pieces = []
        for part in range(fold):
            at = (part * own_pairs + index) * tail
            pieces.append(lanes[:, at : at + tail])
        return jnp.concatenate(pieces, axis=0)

    def unpack(ref, index):
        main = ref[pl.ds(index * width, width), :].astype(F32)
        return jnp.concatenate([main, unpack_tail(ref, index)], axis=1)

    rows_at = lax.broadcasted_iota(jnp.int32, (width, width), 0)
    cols_at = lax.broadcasted_iota(jnp.int32, (width, width), 1)

    def mask_of(row):
        count = count_ref[row]
        keep = (rows_at < count).astype(F32) * (cols_at < count).astype(F32)
        return keep

    orbitals = lax.broadcasted_iota(jnp.int32, occ_ref.shape, 1)

    def occ_of(orbital):
        return jnp.sum(
            jnp.where(orbitals == orbital, occ_ref[...], 0.0), axis=1, keepdims=True
        )

    def denominator_of(row):
        across = jnp.broadcast_to(energy_ref[pl.ds(row, 1), :], (width, width))
        down = jnp.sum(
            jnp.where(rows_at == cols_at, across, 0.0), axis=1, keepdims=True
        )
        return down + across - (occ_of(list_ref[0, row]) + occ_of(list_ref[1, row]))

    @pl.loop(0, n_fit)
    def _(part):
        pack(
            gathered.at[me * n_fit + part],
            [
                mask_of(part * own_pairs + index) * start_ref[part * own_pairs + index]
                for index in range(own_pairs)
            ],
        )

    for index in range(own_pairs):
        row = z * own_pairs + index
        amp_own[index] = mask_of(row) * start_ref[row]

    pl.semaphore_wait(barrier, greeted)

    def direct(owner, part, step, target):
        slot = owner * n_fit + part
        return pltpu.make_async_remote_copy(
            src_ref=gathered.at[slot],
            dst_ref=gathered.at[slot],
            send_sem=gat_send.at[step, part],
            recv_sem=gat_recv.at[slot],
            device_id={"pairs": target, "fit": z},
        )

    def forward(owner, part):
        slot = owner * n_fit + part
        return pltpu.make_async_remote_copy(
            src_ref=gathered.at[slot],
            dst_ref=gathered.at[slot],
            send_sem=gat_fwd.at[slot],
            recv_sem=gat_recv.at[slot],
            device_id={"pairs": sibling, "fit": z},
        )

    relayed = chips == 4
    near = (1, 2) if relayed else ()

    def at_chip(step):
        return flip(chip, step, chips) * 2 + core

    def relay(owner, part, step):
        slot = owner * n_fit + part
        return pltpu.make_async_remote_copy(
            src_ref=gathered.at[slot],
            dst_ref=gathered.at[slot],
            send_sem=gat_relay.at[slot],
            recv_sem=gat_recv.at[slot],
            device_id={"pairs": at_chip(step), "fit": z},
        )

    def send_part(part):
        if relayed:
            for step in near:
                direct(me, part, step, at_chip(step)).start()
        else:

            @pl.loop(1, chips)
            def _(step):
                direct(me, part, step, same_core(step)).start()

        forward(me, part).start()

    def fill(owner, part):
        slot = owner * n_fit + part
        for index in range(own_pairs):
            everything[slot * own_pairs + index] = unpack(
                gathered.at[slot], index
            ).astype(BF16)

    def take_direct(turn):
        part = part_at(turn)
        if relayed:
            for step in near:
                owner = at_chip(step)
                direct(owner, part, step, me).wait_recv()
                if step - 1 == turn % 2:
                    relay(owner, part, 3 - step).start()
                forward(owner, part).start()
            fill(me, part)
            for step in near:
                fill(at_chip(step), part)
        else:
            fill(me, part)

            @pl.loop(1, chips)
            def _(step):
                owner = same_core(chips - step)
                direct(owner, part, step, me).wait_recv()
                forward(owner, part).start()
                fill(owner, part)

    def take_far(turn):
        part = part_at(turn)
        if relayed:
            owner = at_chip(3)
            direct(owner, part, 1, me).wait_recv()
            forward(owner, part).start()
            fill(owner, part)

    def take_sibling():
        @pl.loop(0, n_fit)
        def _(turn):
            part = part_at(turn)

            @pl.loop(0, chips)
            def _(step):
                owner = lax.rem(chip + chips - step, chips) * 2 + (1 - core)
                forward(owner, part).wait_recv()
                fill(owner, part)

    def finish_sends():
        if relayed:
            for turn in range(n_fit):
                part = part_at(turn)
                for step in near:
                    direct(me, part, step, at_chip(step)).wait_send()
                    if step - 1 == turn % 2:
                        relay(at_chip(step), part, 3 - step).wait_send()

        @pl.loop(0, n_fit)
        def _(part):
            @pl.loop(1, chips)
            def _(step):
                if not relayed:
                    direct(me, part, step, same_core(step)).wait_send()
                forward(same_core(step), part).wait_send()

            forward(me, part).wait_send()

    def fit_copy(kind, step, source, target_ref):
        return pltpu.make_async_remote_copy(
            src_ref=source,
            dst_ref=target_ref,
            send_sem=fit_send.at[kind, step],
            recv_sem=fit_recv.at[kind, step],
            device_id={"pairs": me, "fit": part_at(step)},
        )

    def scatter_copy(kind, step, send, recv):
        return fit_copy(kind, step, send.at[step], recv.at[step])

    def spread_copy(kind, step, buffer, slot):
        return fit_copy(kind, step, buffer.at[slot], buffer.at[slot])

    def couple(row):
        coup_own[row] = jnp.zeros((width, width), F32)

        @pl.loop(0, per_pair // GROUP)
        def _(turn):
            total = None
            for inner in range(GROUP):
                col = turn * GROUP + inner
                partner = partner_ref[row, col]
                margin = margins[row, col]
                left = jnp.dot(
                    margin, everything[partner], preferred_element_type=F32
                ).astype(BF16)
                right = lax.dot_general(
                    left,
                    margin,
                    (((1,), (1,)), ((), ())),
                    preferred_element_type=F32,
                )
                term = fock_ref[row, col] * right
                total = term if total is None else total + term
            coup_own[row] = coup_own[row] + total

    INT, COUP, HIGH, LOW, RES = 0, 1, 3, 4, 5

    @pl.loop(0, n_fit)
    def _(part):
        send_part(part_at(part))

    copy_first.wait()
    copy_second.wait()

    def integrals_of(row):
        return lax.dot_general(
            first[row],
            second[row],
            (((1,), (1,)), ((), ())),
            preferred_element_type=F32,
        )

    @pl.loop(1, n_fit)
    def _(step):
        part = part_at(step)
        pack(
            int_send.at[step],
            [integrals_of(part * own_pairs + index) for index in range(own_pairs)],
        )
        scatter_copy(INT, step, int_send, int_recv).start()

    for index in range(own_pairs):
        int_own[index] = integrals_of(z * own_pairs + index)

    @pl.loop(0, pair_dev)
    def _(row):
        denom[row] = denominator_of(row)

    for turn in range(n_fit):
        take_direct(turn)
    for turn in range(n_fit):
        take_far(turn)
    take_sibling()

    for iteration in range(ITERS):
        if iteration == 0:
            for row in range(pair_dev):
                margin_copy(row).wait()
        sent = coup_send.at[iteration]
        got = coup_recv.at[iteration]

        @pl.loop(1, n_fit)
        def _(turn):
            step = n_fit - turn
            part = part_at(step)
            for index in range(own_pairs):
                couple(part * own_pairs + index)
            pack(
                sent.at[step],
                [coup_own[part * own_pairs + index] for index in range(own_pairs)],
            )
            scatter_copy(COUP + iteration, step, sent, got).start()

        for index in range(own_pairs):
            couple(z * own_pairs + index)

        if iteration == 0:
            finish_sends()
            greet(free_sem)

            @pl.loop(1, n_fit)
            def _(step):
                scatter_copy(INT, step, int_send, int_recv).wait()
                for index in range(own_pairs):
                    int_own[index] = int_own[index] + unpack(int_recv.at[step], index)

        @pl.loop(1, n_fit)
        def _(step):
            scatter_copy(COUP + iteration, step, sent, got).wait()
            for index in range(own_pairs):
                row = z * own_pairs + index
                coup_own[row] = coup_own[row] + unpack(got.at[step], index)

        updated, residuals = [], []
        for index in range(own_pairs):
            row = z * own_pairs + index
            denominator = denom[row]
            amplitudes = amp_own[index]
            residual = mask_of(row) * (
                int_own[index] - coup_own[row] + denominator * amplitudes
            )
            residuals.append(residual)
            updated.append(amplitudes - residual / denominator)

        if iteration < ITERS - 1:
            pl.semaphore_wait(free_sem, greeted)
            mine = me * n_fit + z
            pack(gathered.at[mine], updated)
            pack(
                low.at[z],
                [block - block.astype(BF16).astype(F32) for block in updated],
            )
            for step in range(1, n_fit):
                spread_copy(HIGH, step, gathered, mine).start()
            send_part(z)
            for index in range(own_pairs):
                amp_own[index] = updated[index]

            for turn in range(1, n_fit):
                part = part_at(turn)
                spread_copy(HIGH, turn, gathered, me * n_fit + part).wait_recv()
                send_part(part)
                take_direct(turn - 1)
                if turn > 1:
                    take_far(turn - 2)
            for step in range(1, n_fit):
                spread_copy(LOW, step, low, z).start()
            take_direct(n_fit - 1)
            for turn in range(max(n_fit - 2, 0), n_fit):
                take_far(turn)
            take_sibling()
            for step in range(1, n_fit):
                spread_copy(HIGH, step, gathered, mine).wait_send()
        else:
            pack(res_all.at[z], residuals)
            for step in range(1, n_fit):
                spread_copy(RES, step, res_all, z).start()

    finish_sends()
    for step in range(1, n_fit):
        spread_copy(LOW, step, low, z).wait_send()
        part = part_at(step)
        spread_copy(LOW, step, low, part).wait_recv()

    @pl.loop(0, n_fit)
    def _(step):
        part = part_at(step)

        @pl.when(step > 0)
        def _():
            spread_copy(RES, step, res_all, part).wait_recv()

        for index in range(own_pairs):
            row = part * own_pairs + index
            residual = unpack(res_all.at[part], index)
            amplitudes = unpack(gathered.at[me * n_fit + part], index) + unpack(
                low.at[part], index
            )
            res_out[row] = residual
            amp_out[row] = amplitudes - residual / denom[row]

    for step in range(1, n_fit):
        spread_copy(RES, step, res_all, z).wait_send()


GROUP = 12


def shards(
    n_pairs,
    n_fit,
    b_first,
    b_second,
    start_amplitudes,
    margins,
    fock_terms,
    partners,
    pno_energy,
    occ_energy,
    pair_list,
    pno_count,
):
    pair_dev, width, _ = start_amplitudes.shape
    own_pairs = pair_dev // n_fit
    tail = width - LANES
    packed = (own_pairs * width + own_pairs * width * tail // LANES, LANES)
    slots = n_pairs * n_fit
    out = jax.ShapeDtypeStruct(start_amplitudes.shape, F32)
    vmem = pl.BlockSpec(memory_space=pltpu.VMEM)
    smem = pl.BlockSpec(memory_space=pltpu.SMEM)
    hbm = pl.BlockSpec(memory_space=pl.ANY)
    return pl.pallas_call(
        functools.partial(kernel, n_pairs, n_fit),
        out_shape=(out, out),
        in_specs=[vmem, vmem, smem, smem, vmem, smem, smem, hbm, hbm, hbm],
        out_specs=(vmem, vmem),
        scratch_shapes=[
            pltpu.VMEM(margins.shape, BF16),
            pltpu.VMEM(b_first.shape, BF16),
            pltpu.VMEM(b_second.shape, BF16),
            pltpu.VMEM((slots,) + packed, BF16),
            pltpu.VMEM((n_pairs * pair_dev, width, width), BF16),
            pltpu.VMEM((own_pairs, width, width), F32),
            pltpu.VMEM((pair_dev, width, width), F32),
            pltpu.VMEM((n_fit,) + packed, F32),
            pltpu.VMEM((n_fit,) + packed, F32),
            pltpu.VMEM((ITERS, n_fit) + packed, BF16),
            pltpu.VMEM((ITERS, n_fit) + packed, BF16),
            pltpu.VMEM((n_fit,) + packed, BF16),
            pltpu.VMEM((n_fit,) + packed, BF16),
            pltpu.SemaphoreType.DMA((pair_dev,)),
            pltpu.SemaphoreType.DMA((2,)),
            pltpu.SemaphoreType.DMA((n_pairs // 2, n_fit)),
            pltpu.SemaphoreType.DMA((slots,)),
            pltpu.SemaphoreType.DMA((slots,)),
            pltpu.SemaphoreType.DMA((slots,)),
            pltpu.SemaphoreType.DMA((6, n_fit)),
            pltpu.SemaphoreType.DMA((6, n_fit)),
            pltpu.SemaphoreType.REGULAR,
        ],
        compiler_params=pltpu.CompilerParams(
            collective_id=0, has_side_effects=True, vmem_limit_bytes=65000 * 1024
        ),
    )(
        start_amplitudes,
        pno_energy,
        fock_terms,
        partners,
        occ_energy.reshape(1, -1),
        pair_list.T,
        pno_count,
        b_first,
        b_second,
        margins,
    )


def solution(mesh):
    return jax.shard_map(
        functools.partial(shards, mesh.shape["pairs"], mesh.shape["fit"]),
        mesh=mesh,
        in_specs=(
            P("pairs", None, "fit"),
            P("pairs", None, "fit"),
            P("pairs", None, None),
            P("pairs", "fit", None, None),
            P("pairs", "fit"),
            P("pairs", "fit"),
            P("pairs", None),
            P(),
            P("pairs", None),
            P("pairs"),
        ),
        out_specs=(P("pairs", None, None), P("pairs", None, None)),
        check_vma=False,
    )
```
